32 devices in a mesh: grp: 2 (over y), rows: 8 (over z, x), mod: 2 (over core).
Axes of the slice: x: 2, y: 2, z: 4, core: 2. Of those that a mesh axis runs over, the one named last changes fastest.
Arguments:
- queries: bfloat16 [16, 8, 2304], P(('grp', 'rows'), 'mod'), parts along dimension 0, may hold values from -6 to 6
- train_grads: bfloat16 [2048, 8, 2304], P(('grp', 'rows'), 'mod'), parts along dimension 0, may hold values from -6 to 6
- factors: float32 [8, 2, 48, 48], P('mod'), may hold values from -4 to 4, as said below
Outputs:
- scores: float32 [16, 1024], P(('grp', 'mod'), 'rows'), parts along dimension 0
The draws below stay inside these ranges and needn't reach their ends.
There are 2 independent parts, one for each index of `grp`. The reference program is written for one: setup_inputs(seed, part) draws one part's arguments, and reference() takes and returns one part's arrays. A program takes and returns all parts, laid end to end along the dimension named above; an argument that names none is the same for every part. Nothing has to cross between parts.
Inputs may be any that keep to these rules, and one draw needn't show every extreme that they name: `factors`: each factor is a 48 x 48 matrix with a positive diagonal and full rank.
All inputs are finite; a program needn't handle non-finite values.
Results may differ from the reference program's by a relative error of at most 0.0029.
Values may be sent and summed in bfloat16 or wider, within the bound.
No kernel may reach another device: no remote copies, remote signals or barrier semaphores. Data moves between devices by JAX's collectives and lax.ppermute only.
A program may use at most 64 MiB of HBM per device.

```python
import jax
import jax.numpy as jnp
from jax import lax

MODULES = 8
PROJ = 48
T_DEV = 128
COORDS = 2304
NQ = 8
NTRAIN = 1024
N_ROWS = 8


def draw_factors(key, part):
    key_diag, key_off = jax.random.split(jax.random.fold_in(key, 17))
    shape = (MODULES, 2, PROJ, PROJ)
    diag_vals = jnp.exp(jax.random.uniform(key_diag, (MODULES, 2, PROJ), jnp.float32, jnp.log(0.5), jnp.log(2.0)))
    off_vals = jnp.clip(jax.random.normal(key_off, shape, jnp.float32), -4.0, 4.0) * (0.5 / jnp.sqrt(jnp.float32(PROJ)))
    eye_mask = jnp.eye(PROJ, dtype=jnp.float32)
    return off_vals * (1.0 - eye_mask) + diag_vals[..., None] * eye_mask


def levels(stream_key, dims, pieces, least, largest):
    level, own = 1.0, jax.random.fold_in(stream_key, 6)
    for dim, blocks in pieces:
        heights = jnp.exp(jax.random.uniform(jax.random.fold_in(own, dim), (blocks,), jnp.float32, least / len(pieces), largest / len(pieces)))
        level = level * jnp.repeat(heights, dims[dim] // blocks).reshape([-1 if axis == dim else 1 for axis in range(len(dims))])
    return level


def scatter_about(rng, extent, width, limit, pieces=(), kind=jnp.bfloat16):
    entries = width * jax.random.normal(rng, extent, jnp.float32)
    if pieces:
        entries = entries * levels(rng, extent, pieces, -0.22, 0.18)
    return jnp.clip(entries, -limit, limit).astype(kind)


def setup_inputs(seed: int = 0, part: int = 0) -> dict:
    splits = jax.random.split(jax.random.key(seed), 4)
    own_keys = jax.random.split(jax.random.fold_in(splits[3], part), 4)
    queries = scatter_about(own_keys[0], (NQ, MODULES, COORDS), 1.0, 6.0, ((0, 8), (1, 2)))
    train_grads = scatter_about(own_keys[1], (NTRAIN, MODULES, COORDS), 1.0, 6.0, ((0, 8), (1, 2)))
    factors = draw_factors(jax.random.fold_in(splits[3], 71), part)
    return {"queries": queries, "train_grads": train_grads, "factors": factors}


def precondition(queries, factors):
    count = queries.shape[0]
    grads = queries.astype(jnp.float32).reshape(count, MODULES, PROJ, PROJ)
    left_side = jnp.einsum('mab,qmbc->qmac', factors[:, 0], grads, precision=lax.Precision.HIGHEST)
    both_sides = jnp.einsum('qmac,mcd->qmad', left_side, factors[:, 1], precision=lax.Precision.HIGHEST)
    both_sides = both_sides / jnp.sqrt(jnp.float32(MODULES * COORDS))
    return both_sides.astype(jnp.bfloat16).reshape(count, MODULES * COORDS)

def reference(queries, train_grads, factors):
    scaled = precondition(queries, factors)
    blocks = train_grads.reshape(N_ROWS, T_DEV, MODULES * COORDS)

    def score_block(block):
        return lax.dot_general(scaled, block, (((1,), (1,)), ((), ())), preferred_element_type=jnp.float32)
    parts = lax.map(score_block, blocks)
    return jnp.transpose(parts, (1, 0, 2)).reshape(scaled.shape[0], N_ROWS * T_DEV)
```

```python
import jax
import jax.numpy as jnp
from jax import lax
from jax.sharding import PartitionSpec as P

DIRECT_PLANES = 4


def precondition(grads_in, factors):
    count, local_modules, coords = grads_in.shape
    proj = factors.shape[-1]
    modules = local_modules * lax.axis_size("mod")
    grads = grads_in.astype(jnp.float32).reshape(count, local_modules, proj, proj)
    left_side = jnp.einsum("mab,qmbc->qmac", factors[:, 0], grads, precision=lax.Precision.HIGHEST)
    both_sides = jnp.einsum(
        "qmac,mcd->qmad", left_side, factors[:, 1], precision=lax.Precision.HIGHEST
    )
    both_sides = both_sides / jnp.sqrt(jnp.float32(modules * coords))
    return both_sides.astype(jnp.bfloat16).reshape(count, local_modules, coords)


def dot_rows(ready, train_grads):
    return lax.dot_general(
        ready.reshape(ready.shape[0], -1),
        train_grads.reshape(train_grads.shape[0], -1),
        (((1,), (1,)), ((), ())),
        preferred_element_type=jnp.float32,
    )


def send_rows(x, target):
    return lax.ppermute(x, "rows", [(r, target(r)) for r in range(lax.axis_size("rows"))])


def scores_direct(own, train_grads, rows):
    planes = rows // 2
    row = lax.axis_index("rows")
    pair = jnp.concatenate([own, send_rows(own, lambda r: r ^ 1)])
    far = [send_rows(pair, lambda r, s=s: (r + 2 * s) % rows) for s in range(1, planes)]
    part = dot_rows(jnp.concatenate([pair] + far), train_grads)
    count = own.shape[0]
    part = part.reshape(planes, 2, count, -1)
    part = jnp.where(row % 2 == 0, part, part[:, ::-1])
    part = jnp.stack([part[-p % planes] for p in range(planes)])
    step = 1
    while step < planes:
        part = jnp.where((row // 2) & step == 0, part, jnp.roll(part, step, axis=0))
        step *= 2
    part = part.reshape(2, (rows // 2) * count, -1)
    low = lax.axis_index("mod") == 0
    keep, give = jnp.where(low, part[0], part[1]), jnp.where(low, part[1], part[0])
    return keep + lax.ppermute(give, "mod", [(0, 1), (1, 0)])


def scores_gathered(own, train_grads):
    part = dot_rows(lax.all_gather(own, "rows", axis=0, tiled=True), train_grads)
    return lax.psum_scatter(part, "mod", scatter_dimension=0, tiled=True)


def shards(queries, train_grads, factors):
    own = precondition(queries, factors)
    rows = lax.axis_size("rows")
    planes = rows // 2
    if lax.axis_size("mod") == 2 and rows % 2 == 0 and planes <= DIRECT_PLANES and planes & (planes - 1) == 0:
        return scores_direct(own, train_grads, rows)
    return scores_gathered(own, train_grads)


def solution(mesh):
    in_specs = (
        P(("grp", "rows"), "mod", None),
        P(("grp", "rows"), "mod", None),
        P("mod", None, None, None),
    )
    out_specs = P(("grp", "mod"), "rows")
    return jax.shard_map(shards, mesh=mesh, in_specs=in_specs, out_specs=out_specs, check_vma=False)
```

```python
import functools
import math

import jax
import jax.numpy as jnp
import numpy as np
from jax import lax
from jax.experimental import pallas as pl
from jax.experimental.pallas import tpu as pltpu
from jax.sharding import PartitionSpec as P

DIRECT_PLANES = 4

HI = lax.Precision.HIGHEST
NT = (((1,), (1,)), ((), ()))
NN = (((1,), (0,)), ((), ()))


def precondition_kernel(scale, q_hbm, f_hbm, o_ref, q_ref, f_ref, rows_ref, sems):
    copies = [pltpu.make_async_copy(q_hbm, q_ref, sems.at[0])]
    copies += [pltpu.make_async_copy(f_hbm.at[:, j], f_ref.at[:, j], sems.at[2 - j]) for j in (1, 0)]
    for copy in copies:
        copy.start()
    count, local_modules, coords = q_ref.shape
    proj = f_ref.shape[-1]
    width = math.lcm(proj, 128)
    held, groups = width // proj, coords // width
    lane = lax.broadcasted_iota(jnp.int32, (held, width), 1)
    first = lax.broadcasted_iota(jnp.int32, (held, width), 0) * proj
    mine = jnp.logical_and(lane >= first, lane < first + proj)
    column = lax.broadcasted_iota(jnp.int32, (proj, width), 1)
    column = column - column // proj * proj
    pick = (column == lax.broadcasted_iota(jnp.int32, (proj, width), 0)).astype(jnp.bfloat16)
    copies[0].wait()
    spread = []
    for m in range(local_modules):
        for i in range(count):
            row = q_ref[i].astype(jnp.float32)[m : m + 1]
            for g in range(groups):
                part = jnp.broadcast_to(row[:, g * width : (g + 1) * width], (held, width))
                spread.append(jnp.where(mine, part, 0.0))
    spread = jnp.concatenate(spread, axis=0).astype(jnp.bfloat16)
    square = lax.dot_general(spread, pick, NT, preferred_element_type=jnp.float32)
    copies[1].wait()
    copies[2].wait()
    both = []
    for m in range(local_modules):
        right = lax.dot_general(
            square[m * count * proj : (m + 1) * count * proj], f_ref[m, 1], NN,
            precision=HI, preferred_element_type=jnp.float32)
        for i in range(count):
            both.append(lax.dot_general(
                f_ref[m, 0], right[i * proj : (i + 1) * proj], NN,
                precision=HI, preferred_element_type=jnp.float32))
    both = (jnp.concatenate(both, axis=0) / scale).astype(jnp.bfloat16)
    wide = lax.dot_general(both, pick, NN, preferred_element_type=jnp.float32)
    for m in range(local_modules):
        for i in range(count):
            for g in range(groups):
                at = ((m * count + i) * groups + g) * held
                rows_ref[i, m : m + 1, g * width : (g + 1) * width] = jnp.sum(
                    jnp.where(mine, wide[at : at + held], 0.0), axis=0, keepdims=True)
    o_ref[...] = rows_ref[...].astype(jnp.bfloat16)


def precondition(queries, factors, modules):
    scale = np.sqrt(np.float32(modules * queries.shape[2]))
    hbm = pl.BlockSpec(memory_space=pltpu.HBM)
    return pl.pallas_call(
        functools.partial(precondition_kernel, float(scale)),
        out_shape=pltpu.VMEM(queries.shape, jnp.bfloat16),
        in_specs=[hbm, hbm],
        out_specs=pl.BlockSpec(memory_space=pltpu.VMEM),
        scratch_shapes=[
            pltpu.VMEM(queries.shape, queries.dtype),
            pltpu.VMEM(factors.shape, factors.dtype),
            pltpu.VMEM(queries.shape, jnp.float32),
            pltpu.SemaphoreType.DMA((3,)),
        ],
        compiler_params=pltpu.CompilerParams(vmem_limit_bytes=8 << 20),
        name="precondition",
    )(*(pltpu.with_memory_space_constraint(a, pltpu.HBM) for a in (queries, factors)))


def dot_rows(ready, train_grads):
    return lax.dot_general(
        ready, train_grads, (((1, 2), (1, 2)), ((), ())), preferred_element_type=jnp.float32
    )


def send_rows(x, target):
    return lax.ppermute(x, "rows", [(r, target(r)) for r in range(lax.axis_size("rows"))])


def scores_direct(queries, train_grads, factors, modules, rows):
    planes = rows // 2
    row = lax.axis_index("rows")
    own = precondition(queries, factors, modules)
    pair = jnp.concatenate([own, send_rows(own, lambda r: r ^ 1)])
    far = [send_rows(pair, lambda r, s=s: (r + 2 * s) % rows) for s in range(1, planes)]
    part = dot_rows(jnp.concatenate([pair] + far), train_grads)
    count = queries.shape[0]
    part = part.reshape(planes, 2, count, -1)
    part = jnp.where(row % 2 == 0, part, part[:, ::-1])
    part = jnp.stack([part[-p % planes] for p in range(planes)])
    step = 1
    while step < planes:
        part = jnp.where((row // 2) & step == 0, part, jnp.roll(part, step, axis=0))
        step *= 2
    part = part.reshape(2, (rows // 2) * count, -1)
    low = lax.axis_index("mod") == 0
    keep, give = jnp.where(low, part[0], part[1]), jnp.where(low, part[1], part[0])
    return keep + lax.ppermute(give, "mod", [(0, 1), (1, 0)])


def scores_gathered(own, train_grads):
    part = dot_rows(lax.all_gather(own, "rows", axis=0, tiled=True), train_grads)
    return lax.psum_scatter(part, "mod", scatter_dimension=0, tiled=True)


def shards(queries, train_grads, factors):
    modules = queries.shape[1] * lax.axis_size("mod")
    rows = lax.axis_size("rows")
    planes = rows // 2
    if lax.axis_size("mod") == 2 and rows % 2 == 0 and planes <= DIRECT_PLANES and planes & (planes - 1) == 0:
        return scores_direct(queries, train_grads, factors, modules, rows)
    return scores_gathered(precondition(queries, factors, modules), train_grads)


def solution(mesh):
    in_specs = (
        P(("grp", "rows"), "mod", None),
        P(("grp", "rows"), "mod", None),
        P("mod", None, None, None),
    )
    out_specs = P(("grp", "mod"), "rows")
    return jax.shard_map(shards, mesh=mesh, in_specs=in_specs, out_specs=out_specs, check_vma=False)
```

```python
import functools
import math

import jax
import jax.numpy as jnp
import numpy as np
from jax import lax
from jax.experimental import pallas as pl
from jax.experimental.pallas import tpu as pltpu
from jax.sharding import PartitionSpec as P


DIRECT_PLANES = 4

HI = lax.Precision.HIGHEST
NT = (((1,), (1,)), ((), ()))
NN = (((1,), (0,)), ((), ()))


def lane_masks(proj):
    width = math.lcm(proj, 128)
    held = width // proj
    lane = lax.broadcasted_iota(jnp.int32, (held, width), 1)
    first = lax.broadcasted_iota(jnp.int32, (held, width), 0) * proj
    mine = jnp.logical_and(lane >= first, lane < first + proj)
    column = lax.broadcasted_iota(jnp.int32, (proj, width), 1)
    column = column - column // proj * proj
    pick = (column == lax.broadcasted_iota(jnp.int32, (proj, width), 0)).astype(jnp.bfloat16)
    return mine, pick


def squares(query, mine, pick):
    query = query.astype(jnp.float32)
    held, width = mine.shape
    spread = []
    for m in range(query.shape[0]):
        for at in range(0, query.shape[1], width):
            part = jnp.broadcast_to(query[m : m + 1, at : at + width], (held, width))
            spread.append(jnp.where(mine, part, 0.0))
    spread = jnp.concatenate(spread, axis=0).astype(jnp.bfloat16)
    return lax.dot_general(spread, pick, NT, preferred_element_type=jnp.float32)


def both_sides(square, f_ref, scale):
    proj = f_ref.shape[-1]
    both = []
    rights = [lax.dot_general(
        square[m * proj : (m + 1) * proj], f_ref[m, 1], NN,
        precision=HI, preferred_element_type=jnp.float32) for m in range(f_ref.shape[0])]
    for m in range(f_ref.shape[0]):
        both.append(lax.dot_general(
            f_ref[m, 0], rights[m], NN, precision=HI, preferred_element_type=jnp.float32))
    return (jnp.concatenate(both, axis=0) / scale).astype(jnp.bfloat16)


def flatten(both, mine, pick, rows_ref):
    held, width = mine.shape
    wide = lax.dot_general(both, pick, NN, preferred_element_type=jnp.float32)
    at = 0
    for m in range(rows_ref.shape[0]):
        for lanes in range(0, rows_ref.shape[1], width):
            rows_ref[m : m + 1, lanes : lanes + width] = jnp.sum(
                jnp.where(mine, wide[at : at + held], 0.0), axis=0, keepdims=True)
            at += held


def first_kernel(scale, q_hbm, f_hbm, o_ref, f_ref, q_ref, rows_ref, sems):
    copies = [pltpu.make_async_copy(q_hbm, q_ref, sems.at[0])]
    copies += [pltpu.make_async_copy(f_hbm.at[:, j], f_ref.at[:, j], sems.at[2 - j]) for j in (1, 0)]
    for copy in copies:
        copy.start()
    mine, pick = lane_masks(f_ref.shape[-1])
    copies[0].wait()
    for i in range(q_ref.shape[0]):
        square = squares(q_ref[i], mine, pick)
        if i == 0:
            copies[1].wait()
            copies[2].wait()
        flatten(both_sides(square, f_ref, scale), mine, pick, rows_ref)
        o_ref[i] = rows_ref[...].astype(jnp.bfloat16)


def second_kernel(scale, own_ref, q_ref, f_ref, o_ref, rows_ref):
    count = own_ref.shape[0]
    mine, pick = lane_masks(f_ref.shape[-1])
    o_ref[:count] = own_ref[...]
    for i in range(count):
        flatten(both_sides(squares(q_ref[i], mine, pick), f_ref, scale), mine, pick, rows_ref)
        o_ref[count + i] = rows_ref[...].astype(jnp.bfloat16)


def precondition(queries, factors, modules):
    scale = float(np.sqrt(np.float32(modules * queries.shape[2])))
    hbm, vmem = pl.BlockSpec(memory_space=pltpu.HBM), pl.BlockSpec(memory_space=pltpu.VMEM)
    return pl.pallas_call(
        functools.partial(first_kernel, scale),
        out_shape=(pltpu.VMEM(queries.shape, jnp.bfloat16), pltpu.VMEM(factors.shape, factors.dtype)),
        in_specs=[hbm, hbm],
        out_specs=(vmem, vmem),
        scratch_shapes=[
            pltpu.VMEM(queries.shape, queries.dtype),
            pltpu.VMEM(queries.shape[1:], jnp.float32),
            pltpu.SemaphoreType.DMA((3,)),
        ],
        compiler_params=pltpu.CompilerParams(vmem_limit_bytes=8 << 20),
        cost_estimate=pl.CostEstimate(
            flops=24 * queries.size * factors.shape[-1], bytes_accessed=4 * (queries.size + factors.size),
            transcendentals=0),
        name="precondition_own",
    )(*(pltpu.with_memory_space_constraint(a, pltpu.HBM) for a in (queries, factors)))


def precondition_more(own, queries, factors, modules):
    scale = float(np.sqrt(np.float32(modules * queries.shape[2])))
    vmem = pl.BlockSpec(memory_space=pltpu.VMEM)
    return pl.pallas_call(
        functools.partial(second_kernel, scale),
        out_shape=pltpu.VMEM((2 * own.shape[0], *own.shape[1:]), own.dtype),
        in_specs=[vmem] * 3,
        out_specs=vmem,
        scratch_shapes=[pltpu.VMEM(queries.shape[1:], jnp.float32)],
        compiler_params=pltpu.CompilerParams(vmem_limit_bytes=8 << 20),
        name="precondition_neighbour",
    )(own, queries, factors)


def dot_rows(ready, train_grads):
    return lax.dot_general(
        ready, train_grads, (((1, 2), (1, 2)), ((), ())), preferred_element_type=jnp.float32
    )


def send_rows(x, target):
    return lax.ppermute(x, "rows", [(r, target(r)) for r in range(lax.axis_size("rows"))])


def named(x, axes, target):
    return lax.ppermute(x, axes, [(i, target(i)) for i in range(lax.axis_size(axes))])


def scores_direct(queries, train_grads, factors, modules, rows):
    planes = rows // 2
    plane, odd, low = lax.axis_index("rows") // 2, lax.axis_index("rows") % 2, lax.axis_index("mod") == 0
    neighbour = send_rows(queries, lambda r: r ^ 1)
    own, tables = precondition(queries, factors, modules)
    pair = precondition_more(own, neighbour, tables, modules)
    far = [named(pair, ("rows", "mod"), lambda i: ((i // 2 + 2) % rows) * 2 + 1 - i % 2)]
    for s in range(2, planes):
        far.append(named(pair, "rows", lambda r, s=s: (r + 2 * s) % rows))
    far[0] = named(far[0], "mod", lambda c: 1 - c)
    count = queries.shape[0]

    def products(pieces):
        part = dot_rows(jnp.concatenate(pieces), train_grads).reshape(len(pieces), 2, count, -1)
        return jnp.where(odd == 0, part, part[:, ::-1])

    early = products([pair] + far[1:-1])
    early = jnp.concatenate([early[:1], jnp.zeros_like(early[:1]), early[1:], jnp.zeros_like(early[:1])])
    early = jnp.stack([early[-p % planes] for p in range(planes)])
    step = 1
    while step < planes:
        early = jnp.where(plane & step == 0, early, jnp.roll(early, step, axis=0))
        step *= 2
    half = planes // 2
    late = products([far[0], far[-1]])
    place = jnp.arange(half)[:, None, None, None]

    def whole(kept, first):
        where = place + first
        kept = jnp.where(where == (plane - 1) % planes, late[:1], kept)
        kept = jnp.where(where == (plane + 1) % planes, late[1:], kept)
        return kept.reshape(rows // 2 * count, -1)

    keep = whole(jnp.where(low, early[:half], early[half:]), jnp.where(low, 0, half))
    give = whole(jnp.where(low, early[half:], early[:half]), jnp.where(low, half, 0))
    return keep + lax.ppermute(give, "mod", [(0, 1), (1, 0)])


def scores_gathered(own, train_grads):
    part = dot_rows(lax.all_gather(own, "rows", axis=0, tiled=True), train_grads)
    return lax.psum_scatter(part, "mod", scatter_dimension=0, tiled=True)


def goes_direct(rows, cores):
    return cores == 2 and rows == 2 * DIRECT_PLANES


def shards(queries, train_grads, factors):
    modules = queries.shape[1] * lax.axis_size("mod")
    rows = lax.axis_size("rows")
    if goes_direct(rows, lax.axis_size("mod")):
        return scores_direct(queries, train_grads, factors, modules, rows)
    return scores_gathered(precondition(queries, factors, modules)[0], train_grads)


def solution(mesh):
    in_specs = (
        P(("grp", "rows"), "mod", None),
        P(("grp", "rows"), "mod", None),
        P("mod", None, None, None),
    )
    out_specs = P(("grp", "mod"), "rows")
    return jax.shard_map(shards, mesh=mesh, in_specs=in_specs, out_specs=out_specs, check_vma=False)
```

```python
import functools
import math

import jax
import jax.numpy as jnp
import numpy as np
from jax import lax
from jax.experimental import pallas as pl
from jax.experimental.pallas import tpu as pltpu
from jax.sharding import PartitionSpec as P


DIRECT_PLANES = 4

HI = lax.Precision.HIGHEST
NT = (((1,), (1,)), ((), ()))
NN = (((1,), (0,)), ((), ()))


def lane_masks(proj):
    width = math.lcm(proj, 128)
    held = width // proj
    lane = lax.broadcasted_iota(jnp.int32, (held, width), 1)
    first = lax.broadcasted_iota(jnp.int32, (held, width), 0) * proj
    mine = jnp.logical_and(lane >= first, lane < first + proj)
    column = lax.broadcasted_iota(jnp.int32, (proj, width), 1)
    column = column - column // proj * proj
    pick = (column == lax.broadcasted_iota(jnp.int32, (proj, width), 0)).astype(jnp.bfloat16)
    return mine, pick


def squares(query, mine, pick):
    query = query.astype(jnp.float32)
    held, width = mine.shape
    spread = []
    for m in range(query.shape[0]):
        for at in range(0, query.shape[1], width):
            part = jnp.broadcast_to(query[m : m + 1, at : at + width], (held, width))
            spread.append(jnp.where(mine, part, 0.0))
    spread = jnp.concatenate(spread, axis=0).astype(jnp.bfloat16)
    return lax.dot_general(spread, pick, NT, preferred_element_type=jnp.float32)


def both_sides(square, f_ref, scale):
    proj = f_ref.shape[-1]
    both = []
    rights = [lax.dot_general(
        square[m * proj : (m + 1) * proj], f_ref[m, 1], NN,
        precision=HI, preferred_element_type=jnp.float32) for m in range(f_ref.shape[0])]
    for m in range(f_ref.shape[0]):
        both.append(lax.dot_general(
            f_ref[m, 0], rights[m], NN, precision=HI, preferred_element_type=jnp.float32))
    return (jnp.concatenate(both, axis=0) / scale).astype(jnp.bfloat16)


def column_sums(parts):
    row = lax.broadcasted_iota(jnp.int32, parts[0].shape, 0)
    rows = step = len(parts)
    while step > 1:
        step //= 2
        upper = row & step == 0
        joined = []
        for a, b in zip(parts[:step], parts[step:]):
            if 2 * step == rows:
                joined.append(jnp.where(upper, a, b) + pltpu.roll(jnp.where(upper, b, a), step, 0))
            else:
                a, b = a + pltpu.roll(a, rows - step, 0), b + pltpu.roll(b, step, 0)
                joined.append(jnp.where(upper, a, b))
        parts = joined
    return parts[0]


def flatten(both, mine, pick, rows_ref):
    held, width = mine.shape
    modules, coords = rows_ref.shape
    groups = coords // width
    wide = lax.dot_general(both, pick, NN, preferred_element_type=jnp.float32)
    parts = [
        [jnp.where(mine, wide[at : at + held], 0.0) for at in range(m * groups * held, (m + 1) * groups * held, held)]
        for m in range(modules)
    ]
    at = held // modules
    for g in range(0, groups, at):
        sums = column_sums([parts[m][g + i] for i in range(at) for m in range(modules)])
        for i in range(at):
            lanes = slice((g + i) * width, (g + i + 1) * width)
            rows_ref[:, lanes] = sums[i * modules : (i + 1) * modules]


def first_kernel(scale, q_hbm, f_hbm, o_ref, f_ref, q_ref, rows_ref, sems):
    copies = [pltpu.make_async_copy(q_hbm, q_ref, sems.at[0])]
    copies += [pltpu.make_async_copy(f_hbm.at[:, j], f_ref.at[:, j], sems.at[2 - j]) for j in (1, 0)]
    for copy in copies:
        copy.start()
    mine, pick = lane_masks(f_ref.shape[-1])
    copies[0].wait()
    for i in range(q_ref.shape[0]):
        square = squares(q_ref[i], mine, pick)
        if i == 0:
            copies[1].wait()
            copies[2].wait()
        flatten(both_sides(square, f_ref, scale), mine, pick, rows_ref)
        o_ref[i] = rows_ref[...].astype(jnp.bfloat16)


def second_kernel(scale, own_ref, q_ref, f_ref, o_ref, rows_ref):
    count = own_ref.shape[0]
    first = lax.axis_index("rows") % 2 == 0
    mine, pick = lane_masks(f_ref.shape[-1])
    for i in range(count):
        flatten(both_sides(squares(q_ref[i], mine, pick), f_ref, scale), mine, pick, rows_ref)
        own, other = own_ref[i].astype(jnp.float32), rows_ref[...]
        o_ref[i] = jnp.where(first, own, other).astype(jnp.bfloat16)
        o_ref[count + i] = jnp.where(first, other, own).astype(jnp.bfloat16)


def precondition(queries, factors, modules):
    scale = float(np.sqrt(np.float32(modules * queries.shape[2])))
    hbm, vmem = pl.BlockSpec(memory_space=pltpu.HBM), pl.BlockSpec(memory_space=pltpu.VMEM)
    return pl.pallas_call(
        functools.partial(first_kernel, scale),
        out_shape=(pltpu.VMEM(queries.shape, jnp.bfloat16), pltpu.VMEM(factors.shape, factors.dtype)),
        in_specs=[hbm, hbm],
        out_specs=(vmem, vmem),
        scratch_shapes=[
            pltpu.VMEM(queries.shape, queries.dtype),
            pltpu.VMEM(queries.shape[1:], jnp.float32),
            pltpu.SemaphoreType.DMA((3,)),
        ],
        compiler_params=pltpu.CompilerParams(vmem_limit_bytes=8 << 20),
        cost_estimate=pl.CostEstimate(
            flops=24 * queries.size * factors.shape[-1], bytes_accessed=4 * (queries.size + factors.size),
            transcendentals=0),
        name="precondition_own",
    )(*(pltpu.with_memory_space_constraint(a, pltpu.HBM) for a in (queries, factors)))


def precondition_more(own, queries, factors, modules):
    scale = float(np.sqrt(np.float32(modules * queries.shape[2])))
    vmem = pl.BlockSpec(memory_space=pltpu.VMEM)
    return pl.pallas_call(
        functools.partial(second_kernel, scale),
        out_shape=pltpu.VMEM((2 * own.shape[0], *own.shape[1:]), own.dtype),
        in_specs=[vmem] * 3,
        out_specs=vmem,
        scratch_shapes=[pltpu.VMEM(queries.shape[1:], jnp.float32)],
        compiler_params=pltpu.CompilerParams(vmem_limit_bytes=8 << 20),
        name="precondition_neighbour",
    )(own, queries, factors)


def dot_rows(ready, train_grads):
    return lax.dot_general(
        ready, train_grads, (((1, 2), (1, 2)), ((), ())), preferred_element_type=jnp.float32
    )


def send_rows(x, target):
    return lax.ppermute(x, "rows", [(r, target(r)) for r in range(lax.axis_size("rows"))])


def named(x, axes, target):
    return lax.ppermute(x, axes, [(i, target(i)) for i in range(lax.axis_size(axes))])


def scores_direct(queries, train_grads, factors, modules, rows):
    planes = rows // 2
    plane, core = lax.axis_index("rows") // 2, lax.axis_index("mod")
    neighbour = send_rows(queries, lambda r: r ^ 1)
    own, tables = precondition(queries, factors, modules)
    pair = precondition_more(own, neighbour, tables, modules)
    far = [named(pair, ("rows", "mod"), lambda i: ((i // 2 + 2) % rows) * 2 + 1 - i % 2)]
    for s in range(2, planes):
        far.append(named(pair, "rows", lambda r, s=s: (r + 2 * s) % rows))
    back = named(far[0], "mod", lambda c: 1 - c)
    first = back
    half, each = planes // 2, pair.shape[0]

    def planes_of(core):
        at = lax.broadcasted_iota(jnp.int32, (half * each, train_grads.shape[0]), 0)
        return core * half + at // each

    def place(part, i, s, rest, core):
        part = jnp.concatenate([part[i * each : (i + 1) * each]] * half)
        return jnp.where(planes_of(core) == (plane - s) % planes, part, rest)

    early = dot_rows(jnp.concatenate([pair, far[1]]), train_grads)
    late = dot_rows(jnp.concatenate([first, far[2]]), train_grads)

    def whole(core):
        rows_early = place(early, 0, 0, jnp.concatenate([early[each:]] * half), core)
        return place(late, 0, 1, place(late, 1, 3, rows_early, core), core)

    got = lax.ppermute(whole(1 - core), "mod", [(0, 1), (1, 0)])
    return lax.optimization_barrier(whole(core)) + got


def scores_gathered(own, train_grads):
    part = dot_rows(lax.all_gather(own, "rows", axis=0, tiled=True), train_grads)
    return lax.psum_scatter(part, "mod", scatter_dimension=0, tiled=True)


def goes_direct(rows, cores):
    return cores == 2 and rows == 2 * DIRECT_PLANES


def shards(queries, train_grads, factors):
    modules = queries.shape[1] * lax.axis_size("mod")
    rows = lax.axis_size("rows")
    if goes_direct(rows, lax.axis_size("mod")):
        return scores_direct(queries, train_grads, factors, modules, rows)
    return scores_gathered(precondition(queries, factors, modules)[0], train_grads)


def solution(mesh):
    in_specs = (
        P(("grp", "rows"), "mod", None),
        P(("grp", "rows"), "mod", None),
        P("mod", None, None, None),
    )
    out_specs = P(("grp", "mod"), "rows")
    return jax.shard_map(shards, mesh=mesh, in_specs=in_specs, out_specs=out_specs, check_vma=False)
```

```python
import functools
import math

import jax
import jax.numpy as jnp
import numpy as np
from jax import lax
from jax.experimental import pallas as pl
from jax.experimental.pallas import tpu as pltpu
from jax.sharding import PartitionSpec as P


DIRECT_GROUPS = 4

HI = lax.Precision.HIGHEST
NT = (((1,), (1,)), ((), ()))
NN = (((1,), (0,)), ((), ()))


def lane_masks(proj):
    width = math.lcm(proj, 128)
    held = width // proj
    lane = lax.broadcasted_iota(jnp.int32, (held, width), 1)
    first = lax.broadcasted_iota(jnp.int32, (held, width), 0) * proj
    mine = jnp.logical_and(lane >= first, lane < first + proj)
    column = lax.broadcasted_iota(jnp.int32, (proj, width), 1)
    column = column - column // proj * proj
    pick = (column == lax.broadcasted_iota(jnp.int32, (proj, width), 0)).astype(jnp.bfloat16)
    return mine, pick


def squares(query, mine, pick):
    query = query.astype(jnp.float32)
    held, width = mine.shape
    spread = []
    for m in range(query.shape[0]):
        for at in range(0, query.shape[1], width):
            part = jnp.broadcast_to(query[m : m + 1, at : at + width], (held, width))
            spread.append(jnp.where(mine, part, 0.0))
    spread = jnp.concatenate(spread, axis=0).astype(jnp.bfloat16)
    return lax.dot_general(spread, pick, NT, preferred_element_type=jnp.float32)


def split(x):
    parts = []
    for _ in range(3):
        parts.append(x.astype(jnp.bfloat16))
        x = x - parts[-1].astype(jnp.float32)
    return parts


def both_sides(square, f_ref, scale):
    modules, proj = f_ref.shape[0], f_ref.shape[-1]
    square = square.astype(jnp.bfloat16)
    rights = []
    for m in range(modules):
        rows = square[m * proj : (m + 1) * proj]
        rights.append(sum(
            lax.dot_general(rows, part, NN, preferred_element_type=jnp.float32)
            for part in split(f_ref[m, 1])))
    both = [
        lax.dot_general(f_ref[m, 0], rights[m], NN, precision=HI, preferred_element_type=jnp.float32)
        for m in range(modules)
    ]
    return (jnp.concatenate(both, axis=0) / scale).astype(jnp.bfloat16)


def column_sums(parts):
    row = lax.broadcasted_iota(jnp.int32, parts[0].shape, 0)
    rows = step = len(parts)
    while step > 1:
        step //= 2
        upper = row & step == 0
        joined = []
        for a, b in zip(parts[:step], parts[step:]):
            if 2 * step == rows:
                joined.append(jnp.where(upper, a, b) + pltpu.roll(jnp.where(upper, b, a), step, 0))
            else:
                a, b = a + pltpu.roll(a, rows - step, 0), b + pltpu.roll(b, step, 0)
                joined.append(jnp.where(upper, a, b))
        parts = joined
    return parts[0]


def flatten(both, mine, pick, rows_ref):
    held, width = mine.shape
    modules, coords = rows_ref.shape
    groups = coords // width
    wide = lax.dot_general(both, pick, NN, preferred_element_type=jnp.float32)
    parts = [
        [jnp.where(mine, wide[at : at + held], 0.0) for at in range(m * groups * held, (m + 1) * groups * held, held)]
        for m in range(modules)
    ]
    at = held // modules
    for g in range(0, groups, at):
        sums = column_sums([parts[m][g + i] for i in range(at) for m in range(modules)])
        for i in range(at):
            lanes = slice((g + i) * width, (g + i + 1) * width)
            rows_ref[:, lanes] = sums[i * modules : (i + 1) * modules]


def first_kernel(scale, q_hbm, f_hbm, o_ref, f_ref, q_ref, rows_ref, sems):
    copies = [pltpu.make_async_copy(q_hbm, q_ref, sems.at[0])]
    copies += [pltpu.make_async_copy(f_hbm.at[:, j], f_ref.at[:, j], sems.at[2 - j]) for j in (1, 0)]
    for copy in copies:
        copy.start()
    mine, pick = lane_masks(f_ref.shape[-1])
    copies[0].wait()
    for i in range(q_ref.shape[0]):
        square = squares(q_ref[i], mine, pick)
        if i == 0:
            copies[1].wait()
            copies[2].wait()
        flatten(both_sides(square, f_ref, scale), mine, pick, rows_ref)
        o_ref[i] = rows_ref[...].astype(jnp.bfloat16)


def second_kernel(scale, own_ref, q_ref, f_ref, o_ref, rows_ref):
    count = own_ref.shape[0]
    first = lax.axis_index("rows") < lax.axis_size("rows") // 2
    mine, pick = lane_masks(f_ref.shape[-1])
    for i in range(count):
        flatten(both_sides(squares(q_ref[i], mine, pick), f_ref, scale), mine, pick, rows_ref)
        own, other = own_ref[i].astype(jnp.float32), rows_ref[...]
        o_ref[i] = jnp.where(first, own, other).astype(jnp.bfloat16)
        o_ref[count + i] = jnp.where(first, other, own).astype(jnp.bfloat16)


def precondition(queries, factors, modules):
    scale = float(np.sqrt(np.float32(modules * queries.shape[2])))
    hbm, vmem = pl.BlockSpec(memory_space=pltpu.HBM), pl.BlockSpec(memory_space=pltpu.VMEM)
    return pl.pallas_call(
        functools.partial(first_kernel, scale),
        out_shape=(pltpu.VMEM(queries.shape, jnp.bfloat16), pltpu.VMEM(factors.shape, factors.dtype)),
        in_specs=[hbm, hbm],
        out_specs=(vmem, vmem),
        scratch_shapes=[
            pltpu.VMEM(queries.shape, queries.dtype),
            pltpu.VMEM(queries.shape[1:], jnp.float32),
            pltpu.SemaphoreType.DMA((3,)),
        ],
        compiler_params=pltpu.CompilerParams(vmem_limit_bytes=8 << 20),
        cost_estimate=pl.CostEstimate(
            flops=24 * queries.size * factors.shape[-1], bytes_accessed=4 * (queries.size + factors.size),
            transcendentals=0),
        name="precondition_own",
    )(*(pltpu.with_memory_space_constraint(a, pltpu.HBM) for a in (queries, factors)))


def precondition_more(own, queries, factors, modules):
    scale = float(np.sqrt(np.float32(modules * queries.shape[2])))
    vmem = pl.BlockSpec(memory_space=pltpu.VMEM)
    return pl.pallas_call(
        functools.partial(second_kernel, scale),
        out_shape=pltpu.VMEM((2 * own.shape[0], *own.shape[1:]), own.dtype),
        in_specs=[vmem] * 3,
        out_specs=vmem,
        scratch_shapes=[pltpu.VMEM(queries.shape[1:], jnp.float32)],
        compiler_params=pltpu.CompilerParams(vmem_limit_bytes=8 << 20),
        name="precondition_neighbour",
    )(own, queries, factors)


def dot_rows(ready, train_grads):
    return lax.dot_general(
        ready, train_grads, (((1, 2), (1, 2)), ((), ())), preferred_element_type=jnp.float32
    )


def send_rows(x, target):
    return lax.ppermute(x, "rows", [(r, target(r)) for r in range(lax.axis_size("rows"))])


def named(x, axes, target):
    return lax.ppermute(x, axes, [(i, target(i)) for i in range(lax.axis_size(axes))])


def scores_direct(queries, train_grads, factors, modules, rows):
    groups = rows // 2
    group, core = lax.axis_index("rows") % groups, lax.axis_index("mod")
    neighbour = send_rows(queries, lambda r: (r + groups) % rows)
    own, tables = precondition(queries, factors, modules)
    pair = precondition_more(own, neighbour, tables, modules)

    def shifted(r, s):
        return r // groups * groups + (r + s) % groups

    far = [named(pair, ("rows", "mod"), lambda i: shifted(i // 2, 1) * 2 + 1 - i % 2)]
    for s in range(2, groups):
        far.append(named(pair, "rows", lambda r, s=s: shifted(r, s)))
    back = named(far[0], "mod", lambda c: 1 - c)
    count = queries.shape[0]
    owner = lax.broadcasted_iota(jnp.int32, (groups * count, train_grads.shape[0]), 0) // count

    def place(part, i, s, rest, core):
        part = part[2 * i * count : 2 * (i + 1) * count]
        part = jnp.concatenate([jnp.where(core == 0, part[:count], part[count:])] * groups)
        return jnp.where(owner == (group - s) % groups, part, rest)

    early = dot_rows(jnp.concatenate([pair, far[1]]), train_grads)
    late = dot_rows(jnp.concatenate([back, far[2]]), train_grads)

    def whole(core):
        scores = place(early, 1, 2, place(early, 0, 0, 0.0, core), core)
        return place(late, 0, 1, place(late, 1, 3, scores, core), core)

    got = lax.ppermute(whole(1 - core), "mod", [(0, 1), (1, 0)])
    return lax.optimization_barrier(whole(core)) + got


def scores_gathered(own, train_grads):
    part = dot_rows(lax.all_gather(own, "rows", axis=0, tiled=True), train_grads)
    return lax.psum_scatter(part, "mod", scatter_dimension=0, tiled=True)


def goes_direct(rows, cores):
    return cores == 2 and rows == 2 * DIRECT_GROUPS


def shards(queries, train_grads, factors):
    modules = queries.shape[1] * lax.axis_size("mod")
    rows = lax.axis_size("rows")
    if goes_direct(rows, lax.axis_size("mod")):
        return scores_direct(queries, train_grads, factors, modules, rows)
    return scores_gathered(precondition(queries, factors, modules)[0], train_grads)


def solution(mesh):
    in_specs = (
        P(("grp", "rows"), "mod", None),
        P(("grp", "rows"), "mod", None),
        P("mod", None, None, None),
    )
    out_specs = P(("grp", "mod"), "rows")
    return jax.shard_map(shards, mesh=mesh, in_specs=in_specs, out_specs=out_specs, check_vma=False)
```

```python
import functools
import math

import jax
import jax.numpy as jnp
import numpy as np
from jax import lax
from jax.experimental import pallas as pl
from jax.experimental.pallas import tpu as pltpu
from jax.sharding import PartitionSpec as P


DIRECT_GROUPS = 4

HI = lax.Precision.HIGHEST
NT = (((1,), (1,)), ((), ()))
NN = (((1,), (0,)), ((), ()))


def lane_masks(proj):
    width = math.lcm(proj, 128)
    held = width // proj
    lane = lax.broadcasted_iota(jnp.int32, (held, width), 1)
    first = lax.broadcasted_iota(jnp.int32, (held, width), 0) * proj
    mine = jnp.logical_and(lane >= first, lane < first + proj)
    column = lax.broadcasted_iota(jnp.int32, (proj, width), 1)
    column = column - column // proj * proj
    pick = (column == lax.broadcasted_iota(jnp.int32, (proj, width), 0)).astype(jnp.bfloat16)
    return mine, pick


def squares(query, mine, pick):
    query = query.astype(jnp.float32)
    held, width = mine.shape
    spread = []
    for m in range(query.shape[0]):
        for at in range(0, query.shape[1], width):
            part = jnp.broadcast_to(query[m : m + 1, at : at + width], (held, width))
            spread.append(jnp.where(mine, part, 0.0))
    spread = jnp.concatenate(spread, axis=0).astype(jnp.bfloat16)
    return lax.dot_general(spread, pick, NT, preferred_element_type=jnp.float32)


def split(x):
    parts = []
    for _ in range(3):
        parts.append(x.astype(jnp.bfloat16))
        x = x - parts[-1].astype(jnp.float32)
    return parts


def both_sides(square, f_ref, scale):
    modules, proj = f_ref.shape[0], f_ref.shape[-1]
    square = square.astype(jnp.bfloat16)
    rights = []
    for m in range(modules):
        rows = square[m * proj : (m + 1) * proj]
        rights.append(sum(
            lax.dot_general(rows, part, NN, preferred_element_type=jnp.float32)
            for part in split(f_ref[m, 1])))
    both = [
        lax.dot_general(f_ref[m, 0], rights[m], NN, precision=HI, preferred_element_type=jnp.float32)
        for m in range(modules)
    ]
    return (jnp.concatenate(both, axis=0) / scale).astype(jnp.bfloat16)


def column_sums(parts):
    row = lax.broadcasted_iota(jnp.int32, parts[0].shape, 0)
    rows = step = len(parts)
    while step > 1:
        step //= 2
        upper = row & step == 0
        joined = []
        for a, b in zip(parts[:step], parts[step:]):
            if 2 * step == rows:
                joined.append(jnp.where(upper, a, b) + pltpu.roll(jnp.where(upper, b, a), step, 0))
            else:
                a, b = a + pltpu.roll(a, rows - step, 0), b + pltpu.roll(b, step, 0)
                joined.append(jnp.where(upper, a, b))
        parts = joined
    return parts[0]


def flatten(both, mine, pick, rows_ref):
    held, width = mine.shape
    modules, coords = rows_ref.shape
    groups = coords // width
    wide = lax.dot_general(both, pick, NN, preferred_element_type=jnp.float32)
    parts = [
        [jnp.where(mine, wide[at : at + held], 0.0) for at in range(m * groups * held, (m + 1) * groups * held, held)]
        for m in range(modules)
    ]
    at = held // modules
    for g in range(0, groups, at):
        sums = column_sums([parts[m][g + i] for i in range(at) for m in range(modules)])
        for i in range(at):
            lanes = slice((g + i) * width, (g + i + 1) * width)
            rows_ref[:, lanes] = sums[i * modules : (i + 1) * modules]


def first_kernel(scale, q_hbm, f_hbm, o_ref, f_ref, q_ref, rows_ref, sems):
    copies = [pltpu.make_async_copy(q_hbm, q_ref, sems.at[0])]
    copies += [pltpu.make_async_copy(f_hbm.at[:, j], f_ref.at[:, j], sems.at[2 - j]) for j in (1, 0)]
    for copy in copies:
        copy.start()
    mine, pick = lane_masks(f_ref.shape[-1])
    copies[0].wait()
    for i in range(q_ref.shape[0]):
        square = squares(q_ref[i], mine, pick)
        if i == 0:
            copies[1].wait()
            copies[2].wait()
        flatten(both_sides(square, f_ref, scale), mine, pick, rows_ref)
        o_ref[i] = rows_ref[...].astype(jnp.bfloat16)


def second_kernel(scale, own_ref, q_ref, f_ref, o_ref, rows_ref):
    count = own_ref.shape[0]
    place = jnp.where(lax.axis_index("rows") < lax.axis_size("rows") // 2, 0, count)
    mine, pick = lane_masks(f_ref.shape[-1])
    for i in range(count):
        o_ref[place + i] = own_ref[i]
        flatten(both_sides(squares(q_ref[i], mine, pick), f_ref, scale), mine, pick, rows_ref)
        o_ref[count - place + i] = rows_ref[...].astype(jnp.bfloat16)


def precondition(queries, factors, modules):
    scale = float(np.sqrt(np.float32(modules * queries.shape[2])))
    hbm, vmem = pl.BlockSpec(memory_space=pltpu.HBM), pl.BlockSpec(memory_space=pltpu.VMEM)
    return pl.pallas_call(
        functools.partial(first_kernel, scale),
        out_shape=(pltpu.VMEM(queries.shape, jnp.bfloat16), pltpu.VMEM(factors.shape, factors.dtype)),
        in_specs=[hbm, hbm],
        out_specs=(vmem, vmem),
        scratch_shapes=[
            pltpu.VMEM(queries.shape, queries.dtype),
            pltpu.VMEM(queries.shape[1:], jnp.float32),
            pltpu.SemaphoreType.DMA((3,)),
        ],
        compiler_params=pltpu.CompilerParams(vmem_limit_bytes=8 << 20),
        cost_estimate=pl.CostEstimate(
            flops=24 * queries.size * factors.shape[-1], bytes_accessed=4 * (queries.size + factors.size),
            transcendentals=0),
        name="precondition_own",
    )(*(pltpu.with_memory_space_constraint(a, pltpu.HBM) for a in (queries, factors)))


def precondition_more(own, queries, factors, modules):
    scale = float(np.sqrt(np.float32(modules * queries.shape[2])))
    vmem = pl.BlockSpec(memory_space=pltpu.VMEM)
    return pl.pallas_call(
        functools.partial(second_kernel, scale),
        out_shape=pltpu.VMEM((2 * own.shape[0], *own.shape[1:]), own.dtype),
        in_specs=[vmem] * 3,
        out_specs=vmem,
        scratch_shapes=[pltpu.VMEM(queries.shape[1:], jnp.float32)],
        compiler_params=pltpu.CompilerParams(vmem_limit_bytes=8 << 20),
        name="precondition_neighbour",
    )(own, queries, factors)


def dot_rows(ready, train_grads):
    return lax.dot_general(
        ready, train_grads, (((1, 2), (1, 2)), ((), ())), preferred_element_type=jnp.float32
    )


def send_rows(x, target):
    return lax.ppermute(x, "rows", [(r, target(r)) for r in range(lax.axis_size("rows"))])


def named(x, axes, target):
    return lax.ppermute(x, axes, [(i, target(i)) for i in range(lax.axis_size(axes))])


def scores_direct(queries, train_grads, factors, modules, rows):
    groups = rows // 2
    group, core = lax.axis_index("rows") % groups, lax.axis_index("mod")
    neighbour = send_rows(queries, lambda r: (r + groups) % rows)
    own, tables = precondition(queries, factors, modules)
    pair = precondition_more(own, neighbour, tables, modules)

    def shifted(r, s):
        return r // groups * groups + (r + s) % groups

    far = [named(pair, ("rows", "mod"), lambda i: shifted(i // 2, 1) * 2 + 1 - i % 2)]
    for s in range(2, groups):
        far.append(named(pair, "rows", lambda r, s=s: shifted(r, s)))
    back = named(far[0], "mod", lambda c: 1 - c)
    count = queries.shape[0]
    owner = lax.broadcasted_iota(jnp.int32, (groups * count, train_grads.shape[0]), 0) // count

    def place(part, i, s, rest, core):
        part = part[2 * i * count : 2 * (i + 1) * count]
        part = jnp.concatenate([jnp.where(core == 0, part[:count], part[count:])] * groups)
        return jnp.where(owner == (group - s) % groups, part, rest)

    early = dot_rows(jnp.concatenate([pair, far[1]]), train_grads)
    late = dot_rows(jnp.concatenate([back, far[2]]), train_grads)

    def whole(core):
        scores = place(early, 1, 2, place(early, 0, 0, 0.0, core), core)
        return place(late, 0, 1, place(late, 1, 3, scores, core), core)

    got = lax.ppermute(whole(1 - core), "mod", [(0, 1), (1, 0)])
    return lax.optimization_barrier(whole(core)) + got


def scores_gathered(own, train_grads):
    part = dot_rows(lax.all_gather(own, "rows", axis=0, tiled=True), train_grads)
    return lax.psum_scatter(part, "mod", scatter_dimension=0, tiled=True)


def goes_direct(rows, cores):
    return cores == 2 and rows == 2 * DIRECT_GROUPS


def shards(queries, train_grads, factors):
    modules = queries.shape[1] * lax.axis_size("mod")
    rows = lax.axis_size("rows")
    if goes_direct(rows, lax.axis_size("mod")):
        return scores_direct(queries, train_grads, factors, modules, rows)
    return scores_gathered(precondition(queries, factors, modules)[0], train_grads)


def solution(mesh):
    in_specs = (
        P(("grp", "rows"), "mod", None),
        P(("grp", "rows"), "mod", None),
        P("mod", None, None, None),
    )
    out_specs = P(("grp", "mod"), "rows")
    return jax.shard_map(shards, mesh=mesh, in_specs=in_specs, out_specs=out_specs, check_vma=False)
```
